32 devices in a mesh: tile: 4 (over y, core), mem: 8 (over z, x).
Axes of the slice: x: 2, y: 2, z: 4, core: 2. Of those that a mesh axis runs over, the one named last changes fastest.
Arguments:
- perturbations: bfloat16 [16, 12, 64, 512], P('mem', None, None, 'tile'), may hold values from -6 to 6
- increment: float32 [12, 64, 512], P(None, 'mem', 'tile'), may hold values from -6 to 6
- kappa_east: float32 [64, 512], P('mem', 'tile'), may hold values from 0.02 to 0.16
- kappa_north: float32 [64, 512], P('mem', 'tile'), may hold values from 0.02 to 0.16
- kappa_vertical: float32 [64, 512], P('mem', 'tile'), may hold values from 0.02 to 0.16
- cell_area: float32 [64, 512], P('mem', 'tile'), may hold values from 1 to 2
- norm_weight: float32 [64, 512], P('mem', 'tile'), may hold values from 0.5 to 2
- bottom_level: int32 [64, 512], P('mem', 'tile'), may hold values from 0 to 12
Outputs:
- covariance_product: float32 [12, 64, 512], P(None, 'mem', 'tile')
The draws below stay inside these ranges and needn't reach their ends.
Inputs may be any that keep to these rules, and one draw needn't show every extreme that they name: A column has ocean at levels below its bottom_level; 0 marks a land column.
All inputs are finite; a program needn't handle non-finite values.
Results may differ from the reference program's by a relative error of at most 0.0008.
Values may be sent and summed in bfloat16 or wider, within the bound.
No kernel may reach another device: no remote copies, remote signals or barrier semaphores. Data moves between devices by JAX's collectives and lax.ppermute only.
A program may use at most 64 MiB of HBM per device.

```python
import math
import jax
import jax.numpy as jnp
from jax import lax

NZ = 12
STEPS = 4
MEMBERS = 16
NX = 512
NY = 64


def plant(values, own_key, least, top_value):
    place = [jax.random.randint(jax.random.fold_in(own_key, axis), (), 0, length) for axis, length in enumerate(values.shape)]
    longest = values.shape.index(max(values.shape))
    next_to = place[:longest] + [(place[longest] + 1) % values.shape[longest]] + place[longest + 1:]
    return values.at[tuple(place)].set(least).at[tuple(next_to)].set(top_value)


def steps_of(rng, dims, shards, least, largest):
    def one(dim, parts):
        steps = jax.random.uniform(jax.random.fold_in(jax.random.fold_in(rng, 6), dim), (parts,), jnp.float32, least / len(shards), largest / len(shards))
        return jnp.repeat(jnp.exp(steps), dims[dim] // parts).reshape((-1,) + (1,) * (len(dims) - dim - 1))

    gain = one(*shards[0])
    for cut in shards[1:]:
        gain = gain * one(*cut)
    return gain


def normal_values(key, shape, deviation, limit, pieces=(), dtype=jnp.bfloat16):
    level = steps_of(key, shape, pieces, -0.22, 0.18) if pieces else 1.0
    array = jax.random.normal(key, shape, jnp.float32) * deviation * level
    return jnp.minimum(jnp.maximum(array, -limit), limit).astype(dtype)


def setup_inputs(seed: int = 0) -> dict:
    seeds = jax.random.split(jax.random.key(seed), 9)
    return {
        "perturbations": normal_values(seeds[0], (MEMBERS, NZ, NY, NX), 1.0, 6.0, ((0, 8), (3, 4))),
        "increment": normal_values(seeds[1], (NZ, NY, NX), 1.0, 6.0, ((1, 8), (2, 4)), jnp.float32),
        "kappa_east": jnp.clip(jnp.exp(math.log(0.16) - 2.0794415 * jax.random.uniform(seeds[2], (NY, NX), jnp.float32) ** steps_of(seeds[2], (NY, NX), ((0, 8), (1, 4)), -0.2, 0.2)), 0.02, 0.16),
        "kappa_north": jnp.clip(jnp.exp(math.log(0.16) - 2.0794415 * jax.random.uniform(seeds[3], (NY, NX), jnp.float32) ** steps_of(seeds[3], (NY, NX), ((0, 8), (1, 4)), -0.2, 0.2)), 0.02, 0.16),
        "kappa_vertical": jnp.clip(jnp.exp(math.log(0.16) - 2.0794415 * jax.random.uniform(seeds[4], (NY, NX), jnp.float32) ** steps_of(seeds[4], (NY, NX), ((0, 8), (1, 4)), -0.2, 0.2)), 0.02, 0.16),
        "cell_area": jnp.clip(1.0 + 1.0 * jax.random.uniform(seeds[5], (NY, NX), jnp.float32) ** steps_of(seeds[5], (NY, NX), ((0, 8), (1, 4)), -0.2, 0.2), 1.0, 2.0),
        "norm_weight": jnp.clip(jnp.exp(math.log(2.0) - 1.3862944 * jax.random.uniform(seeds[6], (NY, NX), jnp.float32) ** steps_of(seeds[6], (NY, NX), ((0, 8), (1, 4)), -0.2, 0.2)), 0.5, 2.0),
        "bottom_level": plant(jax.random.randint(seeds[7], (NY, NX), 0, NZ + 1), jax.random.fold_in(seeds[7], 1), 0, NZ).astype(jnp.int32),
    }


def face_weights(east_pad, north_pad, bottom_pad, kappa_up):
    levels = lax.broadcasted_iota(jnp.float32, (NZ, 1, 1), 0)
    ocean_pad = (levels < bottom_pad[None]).astype(jnp.float32)
    east_faces = east_pad[None, 1:-1, :-1] * ocean_pad[:, 1:-1, :-1] * ocean_pad[:, 1:-1, 1:]
    north_faces = north_pad[None, :-1, 1:-1] * ocean_pad[:, :-1, 1:-1] * ocean_pad[:, 1:, 1:-1]
    ocean = ocean_pad[:, 1:-1, 1:-1]
    upper_faces = kappa_up[None] * ocean[:-1] * ocean[1:]
    return ocean, east_faces, north_faces, upper_faces


def divergence(padded, east_faces, north_faces, upper_faces):
    centre = padded[..., 1:-1, 1:-1]
    east_flux = east_faces[:, :, 1:] * (padded[..., 1:-1, 2:] - centre)
    west_flux = east_faces[:, :, :-1] * (centre - padded[..., 1:-1, :-2])
    north_flux = north_faces[:, 1:, :] * (padded[..., 2:, 1:-1] - centre)
    south_flux = north_faces[:, :-1, :] * (centre - padded[..., :-2, 1:-1])
    vertical = upper_faces * (centre[..., 1:, :, :] - centre[..., :-1, :, :])
    nothing = jnp.zeros_like(vertical[..., :1, :, :])
    above = jnp.concatenate([vertical, nothing], axis=-3)
    below = jnp.concatenate([nothing, vertical], axis=-3)
    return east_flux - west_flux + north_flux - south_flux + above - below


def pad_plain(tracer):
    return jnp.pad(tracer, ((0, 0), (1, 1), (1, 1)))


def reference(perturbations, increment, kappa_east, kappa_north, kappa_vertical, cell_area, norm_weight, bottom_level):
    ocean, east_faces, north_faces, upper_faces = face_weights(
        jnp.pad(kappa_east, 1), jnp.pad(kappa_north, 1),
        jnp.pad(bottom_level.astype(jnp.float32), 1), kappa_vertical)
    weight = ocean * norm_weight[None]
    scaled = weight * increment

    def add_member(summed, member):
        member_f = member.astype(jnp.float32)
        tracer = member_f * scaled
        for iteration in range(STEPS):
            tracer = tracer + divergence(pad_plain(tracer / cell_area), east_faces, north_faces, upper_faces)
        for iteration in range(STEPS):
            tracer = tracer + divergence(pad_plain(tracer), east_faces, north_faces, upper_faces) / cell_area
        return summed + member_f * weight * tracer, None

    summed, unused = lax.scan(add_member, jnp.zeros(increment.shape, jnp.float32), perturbations)
    return summed / (MEMBERS - 1)
```

```python
import functools

import jax
import jax.numpy as jnp
from jax import lax
from jax.experimental import pallas as pl
from jax.experimental.pallas import tpu as pltpu
from jax.sharding import PartitionSpec as P

NZ = 12
STEPS = 4
HALO = 2 * STEPS
PLANES = NZ + 4
ROWS = 8


def vmem(count):
    return [pl.BlockSpec(memory_space=pltpu.VMEM)] * count


def pack_kernel(inc, east, north, up, area, norm, bottom, out):
    levels = bottom[...].astype(jnp.float32)
    weight = norm[...]
    for z in range(NZ):
        out[z] = jnp.where(levels > z, weight * inc[z], 0.0)
    out[NZ] = east[...]
    out[NZ + 1] = north[...]
    out[NZ + 2] = up[...]
    out[NZ + 3] = area[...] + 4.0 * levels


def unpack(packed):
    levels = jnp.floor(packed * 0.25)
    return jnp.maximum(packed - 4.0 * levels, 1.0), levels


def spread_kernel(count, width, *refs):
    origin = refs[0]
    blocks = refs[1 : 1 + count]
    members, fields, start, coefs, low, high, whole = refs[1 + count :]
    groups = fields.shape[0]
    copies = members.shape[0] // groups
    for k in range(count):
        row = pl.multiple_of(origin[k] * ROWS, ROWS)
        for q in range(PLANES):
            whole[q, pl.ds(row, ROWS), :] = blocks[k][q]

    def turned(q):
        plane = whole[q]
        return jnp.concatenate([plane] * copies, axis=0).T

    packed = turned(PLANES - 1)
    area, unused = unpack(packed)
    inverse = 1.0 / area

    def edges(q, value):
        low[q] = value[:HALO]
        high[q] = value[width - HALO :]

    for q in range(4):
        value = packed if q == 3 else turned(NZ + q)
        coefs[q] = value
        edges(groups * NZ + q, value)
    for z in range(NZ):
        scaled = turned(z) * inverse
        for g in range(groups):
            rows = [members[g * copies + m, z].astype(jnp.float32) for m in range(copies)]
            field = jnp.concatenate(rows, axis=0).T
            fields[g, z] = field
            first = field * scaled
            start[g, z] = first
            edges(g * NZ + z, first)


def diffuse_kernel(count, rows, fields, start, coefs, low, high, out, ping, pong, mid, east, west, north, south, upper, flat, final):
    groups, nz, width, lanes = start.shape
    pad = HALO
    tiles = width // HALO + 2
    total = width + 2 * HALO
    zero = jnp.zeros((pad, lanes), jnp.float32)

    def widen(ref, index, left, inner, right):
        ref[(*index, slice(0, pad))] = zero
        ref[(*index, slice(pad, 2 * pad))] = left
        ref[(*index, slice(2 * pad, 2 * pad + width))] = inner
        ref[(*index, slice(2 * pad + width, 3 * pad + width))] = right
        ref[(*index, slice(pad + total, 2 * pad + total))] = zero

    for g in range(groups):
        for z in range(NZ):
            widen(ping, (g, z), low[g * NZ + z], start[g, z], high[g * NZ + z])
            pong[g, z, 0:pad] = zero
            pong[g, z, pad + total : 2 * pad + total] = zero
    for q in range(4):
        widen(flat, (q,), low[groups * NZ + q], coefs[q], high[groups * NZ + q])
    lane = lax.broadcasted_iota(jnp.int32, (HALO, lanes), 1)
    last = lane % rows == rows - 1

    def shifted(ref, q, first, offset):
        return ref[q, pl.ds(first + offset, HALO), :]

    def weights(tile, carry):
        first = pl.multiple_of(pad + tile * HALO, HALO)
        area, levels = unpack(shifted(flat, 3, first, 0))
        unused, levels_east = unpack(shifted(flat, 3, first, 1))
        unused, levels_west = unpack(shifted(flat, 3, first, -1))
        inverse = 1.0 / area
        levels_north = pltpu.roll(levels, lanes - 1, 1)
        east_w = shifted(flat, 0, first, 0) * inverse
        west_w = shifted(flat, 0, first, -1) * inverse
        face = jnp.where(last, 0.0, shifted(flat, 1, first, 0))
        depth = jnp.minimum(levels, levels_north)
        depth_south = pltpu.roll(depth, 1, 1)
        north_w = face * inverse
        south_w = pltpu.roll(face, 1, 1) * inverse
        up_w = shifted(flat, 2, first, 0) * inverse
        depth_east = jnp.minimum(levels, levels_east)
        depth_west = jnp.minimum(levels, levels_west)
        below = jnp.zeros((HALO, lanes), jnp.float32)
        for z in range(NZ):
            e = jnp.where(depth_east > z, east_w, 0.0)
            w = jnp.where(depth_west > z, west_w, 0.0)
            n = jnp.where(depth > z, north_w, 0.0)
            s = jnp.where(depth_south > z, south_w, 0.0)
            a = jnp.where(levels > z + 1, up_w, 0.0)
            east[z, pl.ds(first, HALO), :] = e
            west[z, pl.ds(first, HALO), :] = w
            north[z, pl.ds(first, HALO), :] = n
            south[z, pl.ds(first, HALO), :] = s
            upper[z, pl.ds(first, HALO), :] = a
            mid[z, pl.ds(first, HALO), :] = 1.0 - (e + w + n + s + a + below)
            below = a
        return carry

    lax.fori_loop(0, tiles, weights, 0)

    def step(source, target, turn):
        def body(g, tile):
            first = pl.multiple_of(pad + tile * HALO, HALO)
            here = pl.ds(first, HALO)
            centre = source[g, 0, here, :]
            under = None
            up_w = None
            if turn == STEPS - 1:
                area, unused = unpack(flat[3, here, :])
            for z in range(NZ):
                total = mid[z, here, :] * centre
                total += east[z, here, :] * source[g, z, pl.ds(first + 1, HALO), :]
                total += west[z, here, :] * source[g, z, pl.ds(first - 1, HALO), :]
                total += north[z, here, :] * pltpu.roll(centre, lanes - 1, 1)
                total += south[z, here, :] * pltpu.roll(centre, 1, 1)
                if z > 0:
                    total += up_w * under
                under = centre
                if z < NZ - 1:
                    up_w = upper[z, here, :]
                    centre = source[g, z + 1, here, :]
                    total += up_w * centre
                if turn == STEPS - 1:
                    total = total * area
                if turn == 2 * STEPS - 1:
                    inner = pl.ds(pl.multiple_of(tile * HALO - HALO, HALO), HALO)
                    final[g, z, inner, :] = total * fields[g, z, inner, :]
                else:
                    target[g, z, here, :] = total

        edge = 1 if turn == 2 * STEPS - 1 else 0
        for g in range(groups):

            @pl.loop(edge, tiles - edge)
            def sweep(tile):
                body(g, tile)

    for turn in range(2 * STEPS):
        source, target = (ping, pong) if turn % 2 == 0 else (pong, ping)
        step(source, target, turn)
    for z in range(NZ):
        parts = []
        for g in range(groups):
            turned = final[g, z].T
            parts += [turned[first : first + rows] for first in range(0, lanes, rows)]
        summed = parts[0]
        for part in parts[1:]:
            summed = summed + part
        for r in range(count):
            out[r, z * ROWS : (z + 1) * ROWS, :] = summed[r * ROWS : (r + 1) * ROWS].astype(out.dtype)


def local(perturbations, increment, kappa_east, kappa_north, kappa_vertical, cell_area, norm_weight, bottom_level):
    count = lax.axis_size("mem")
    me = lax.axis_index("mem")
    sides = lax.axis_size("tile")
    copies, nz, rows, width = perturbations.shape
    lanes = 128
    groups = copies * rows // lanes
    f32 = jnp.float32
    shape = jax.ShapeDtypeStruct
    params = pltpu.CompilerParams(vmem_limit_bytes=56 * 2**20)

    packed = pl.pallas_call(
        pack_kernel,
        out_shape=shape((PLANES, ROWS, width), f32),
        in_specs=vmem(7),
        out_specs=vmem(1)[0],
    )(increment, kappa_east, kappa_north, kappa_vertical, cell_area, norm_weight, bottom_level)

    def turn(x, k):
        return lax.ppermute(x, "mem", [(i, (i + k) % count) for i in range(count)])

    blocks = [packed] + [turn(packed, k) for k in range(1, count)]
    origin = (me - jnp.arange(count, dtype=jnp.int32)) % count

    fields, start, coefs, low, high = pl.pallas_call(
        functools.partial(spread_kernel, count, width),
        out_shape=(
            shape((groups, NZ, width, lanes), f32),
            shape((groups, NZ, width, lanes), f32),
            shape((4, width, lanes), f32),
            shape((groups * NZ + 4, HALO, lanes), f32),
            shape((groups * NZ + 4, HALO, lanes), f32),
        ),
        in_specs=[pl.BlockSpec(memory_space=pltpu.SMEM)] + vmem(count + 1),
        out_specs=tuple(vmem(5)),
        scratch_shapes=[pltpu.VMEM((PLANES, rows, width), f32)],
        compiler_params=params,
    )(origin, *blocks, perturbations)

    from_left = lax.ppermute(high, "tile", [(i, i + 1) for i in range(sides - 1)])
    from_right = lax.ppermute(low, "tile", [(i + 1, i) for i in range(sides - 1)])

    tall = width + 4 * HALO
    state = pltpu.VMEM((groups, NZ, tall, lanes), f32)
    big = pltpu.VMEM((NZ, tall, lanes), f32)
    parts = pl.pallas_call(
        functools.partial(diffuse_kernel, count, rows),
        out_shape=shape((count, NZ * ROWS, width), f32),
        in_specs=vmem(5),
        out_specs=vmem(1)[0],
        scratch_shapes=[state] * 2 + [big] * 6 + [pltpu.VMEM((4, tall, lanes), f32), pltpu.VMEM((groups, NZ, width, lanes), f32)],
        compiler_params=params,
    )(fields, start, coefs, from_left, from_right)

    summed = lax.dynamic_index_in_dim(parts, me, 0, keepdims=False).astype(f32)
    for k in range(1, count):
        piece = lax.dynamic_index_in_dim(parts, (me + k) % count, 0, keepdims=False)
        summed = summed + turn(piece, k).astype(f32)
    summed = summed.reshape(NZ, ROWS, width)
    level = lax.broadcasted_iota(jnp.int32, (NZ, 1, 1), 0)
    weight = jnp.where(level < bottom_level[None], norm_weight[None], 0.0)
    return summed * weight / (copies * count - 1)


def solution(mesh):
    flat = P("mem", "tile")
    deep = P(None, "mem", "tile")
    return jax.shard_map(
        local,
        mesh=mesh,
        in_specs=(P("mem", None, None, "tile"), deep, flat, flat, flat, flat, flat, flat),
        out_specs=deep,
        check_vma=False,
    )
```

```python
import functools

import jax
import jax.numpy as jnp
from jax import lax
from jax.experimental import pallas as pl
from jax.experimental.pallas import tpu as pltpu
from jax.sharding import PartitionSpec as P

NZ = 12
STEPS = 4
HALO = 2 * STEPS
PLANES = NZ + 4
ROWS = 8
UNROLL = 9


def vmem(count):
    return [pl.BlockSpec(memory_space=pltpu.VMEM)] * count


def pack_kernel(share, inc, east, north, up, area, norm, bottom, out, factor):
    levels = bottom[...].astype(jnp.float32)
    weight = norm[...]
    for z in range(NZ):
        out[z] = jnp.where(levels > z, weight * inc[z], 0.0)
        factor[z * ROWS : (z + 1) * ROWS] = jnp.where(levels > z, weight * share, 0.0)
    out[NZ] = east[...]
    out[NZ + 1] = north[...]
    out[NZ + 2] = up[...]
    out[NZ + 3] = area[...] + 4.0 * levels


def unpack(packed):
    levels = jnp.floor(packed * 0.25)
    return jnp.maximum(packed - 4.0 * levels, 1.0), levels


def turn_kernel(members, fields):
    groups = fields.shape[0]
    copies = members.shape[0] // groups
    for g in range(groups):
        for z in range(NZ):
            rows = [members[g * copies + m, z].astype(jnp.float32) for m in range(copies)]
            fields[g, z] = jnp.concatenate(rows, axis=0).T


def spread_kernel(count, width, copies, *refs):
    half = count // 2
    blocks = refs[:half]
    fields, start, coefs, near, far, whole = refs[half:]
    groups = fields.shape[0]
    me = lax.axis_index("mem")
    even = lax.rem(lax.axis_index("tile"), 2) == 0
    for k in range(half):
        for h in range(2):
            row = pl.multiple_of((me ^ (k + h * half)) * ROWS, ROWS)
            for q in range(PLANES):
                whole[q, pl.ds(row, ROWS), :] = blocks[k][h, q]

    def turned(q):
        plane = whole[q]
        return jnp.concatenate([plane] * copies, axis=0).T

    packed = turned(PLANES - 1)
    area, unused = unpack(packed)
    inverse = 1.0 / area

    def edges(q, value):
        low, high = value[:HALO], value[width - HALO :]
        near[q] = jnp.where(even, high, low)
        far[q] = jnp.where(even, low, high)

    for q in range(4):
        value = packed if q == 3 else turned(NZ + q)
        coefs[q] = value
        edges(groups * NZ + q, value)
    for z in range(NZ):
        scaled = turned(z) * inverse
        for g in range(groups):
            first = fields[g, z] * scaled
            start[g, z] = first
            edges(g * NZ + z, first)


def diffuse_kernel(count, rows, sides, fields, start, coefs, near, far, *refs):
    half = count // 2
    outs = refs[:half]
    ping, pong, mid, east, flat, plane, final, joined = refs[half:]
    groups, nz, width, lanes = start.shape
    pad = HALO
    me = lax.axis_index("mem")
    tile = lax.axis_index("tile")
    even = lax.rem(tile, 2) == 0
    first_tile = tile == 0
    last_tile = tile == sides - 1

    def left(q):
        return jnp.where(first_tile, 0.0, jnp.where(even, far[q], near[q]))

    def right(q):
        return jnp.where(last_tile, 0.0, jnp.where(even, near[q], far[q]))

    tiles = width // HALO + 2
    total = width + 2 * HALO
    zero = jnp.zeros((pad, lanes), jnp.float32)

    def widen(ref, index, before, inner, after):
        ref[(*index, slice(0, pad))] = zero
        ref[(*index, slice(pad, 2 * pad))] = before
        ref[(*index, slice(2 * pad, 2 * pad + width))] = inner
        ref[(*index, slice(2 * pad + width, 3 * pad + width))] = after
        ref[(*index, slice(pad + total, 2 * pad + total))] = zero

    for g in range(groups):
        for z in range(NZ):
            widen(ping, (g, z), left(g * NZ + z), start[g, z], right(g * NZ + z))
            pong[g, z, 0:pad] = zero
            pong[g, z, pad + total : 2 * pad + total] = zero
    for q in range(4):
        widen(flat, (q,), left(groups * NZ + q), coefs[q], right(groups * NZ + q))
    lane = lax.broadcasted_iota(jnp.int32, (HALO, lanes), 1)
    last = lane % rows == rows - 1

    def shifted(ref, q, first, offset):
        return ref[q, pl.ds(first + offset, HALO), :]

    def weights(tile, carry):
        first = pl.multiple_of(pad + tile * HALO, HALO)
        area, levels = unpack(shifted(flat, 3, first, 0))
        unused, levels_east = unpack(shifted(flat, 3, first, 1))
        unused, levels_west = unpack(shifted(flat, 3, first, -1))
        inverse = 1.0 / area
        levels_north = pltpu.roll(levels, lanes - 1, 1)
        east_w = shifted(flat, 0, first, 0) * inverse
        west_w = shifted(flat, 0, first, -1) * inverse
        face = jnp.where(last, 0.0, shifted(flat, 1, first, 0))
        depth = jnp.minimum(levels, levels_north)
        depth_south = pltpu.roll(depth, 1, 1)
        north_w = face * inverse
        south_w = pltpu.roll(face, 1, 1) * inverse
        up_w = shifted(flat, 2, first, 0) * inverse
        depth_east = jnp.minimum(levels, levels_east)
        depth_west = jnp.minimum(levels, levels_west)
        here = pl.ds(first, HALO)
        for q, value in enumerate((west_w, north_w, south_w, up_w, depth_west, depth, depth_south, levels, area)):
            plane[q, here, :] = value
        below = jnp.zeros((HALO, lanes), jnp.float32)
        for z in range(NZ):
            e = jnp.where(depth_east > z, east_w, 0.0)
            w = jnp.where(depth_west > z, west_w, 0.0)
            n = jnp.where(depth > z, north_w, 0.0)
            s = jnp.where(depth_south > z, south_w, 0.0)
            a = jnp.where(levels > z + 1, up_w, 0.0)
            east[z, here, :] = e
            mid[z, here, :] = 1.0 - (e + w + n + s + a + below)
            below = a
        return carry

    lax.fori_loop(0, tiles, weights, 0)

    def step(source, target, turn):
        def body(g, tile):
            first = pl.multiple_of(pad + tile * HALO, HALO)
            here = pl.ds(first, HALO)
            west_w, north_w, south_w, up_w, depth_west, depth, depth_south, levels = [plane[q, here, :] for q in range(8)]
            if turn == STEPS - 1:
                area = plane[8, here, :]
            centre = source[g, 0, here, :]
            under = None
            link = None
            for z in range(NZ):
                total = mid[z, here, :] * centre
                total += east[z, here, :] * source[g, z, pl.ds(first + 1, HALO), :]
                total += jnp.where(depth_west > z, west_w, 0.0) * source[g, z, pl.ds(first - 1, HALO), :]
                total += jnp.where(depth > z, north_w, 0.0) * pltpu.roll(centre, lanes - 1, 1)
                total += jnp.where(depth_south > z, south_w, 0.0) * pltpu.roll(centre, 1, 1)
                if z > 0:
                    total += link * under
                under = centre
                if z < NZ - 1:
                    link = jnp.where(levels > z + 1, up_w, 0.0)
                    centre = source[g, z + 1, here, :]
                    total += link * centre
                if turn == STEPS - 1:
                    total = total * area
                if turn == 2 * STEPS - 1:
                    inner = pl.ds(pl.multiple_of(tile * HALO - HALO, HALO), HALO)
                    final[g, z, inner, :] = total * fields[g, z, inner, :]
                else:
                    target[g, z, here, :] = total

        edge = 1 if turn == 2 * STEPS - 1 else 0
        for g in range(groups):

            run = max(r for r in range(1, UNROLL + 1) if (tiles - 2 * edge) % r == 0)

            @pl.loop(0, (tiles - 2 * edge) // run)
            def sweep(turn_of):
                for k in range(run):
                    body(g, edge + turn_of * run + k)

    for turn in range(2 * STEPS):
        source, target = (ping, pong) if turn % 2 == 0 else (pong, ping)
        step(source, target, turn)
    for z in range(NZ):
        parts = []
        for g in range(groups):
            turned = final[g, z].T
            parts += [turned[first : first + rows] for first in range(0, lanes, rows)]
        summed = parts[0]
        for part in parts[1:]:
            summed = summed + part
        joined[z] = summed
    for k in range(half):
        for h in range(2):
            row = pl.multiple_of((me ^ (k + h * half)) * ROWS, ROWS)
            for z in range(NZ):
                outs[k][h, z * ROWS : (z + 1) * ROWS, :] = joined[z, pl.ds(row, ROWS), :]


def local(perturbations, increment, kappa_east, kappa_north, kappa_vertical, cell_area, norm_weight, bottom_level):
    count = lax.axis_size("mem")
    sides = lax.axis_size("tile")
    copies, nz, rows, width = perturbations.shape
    lanes = 128
    groups = copies * rows // lanes
    half = count // 2
    f32 = jnp.float32
    shape = pltpu.VMEM
    params = pltpu.CompilerParams(vmem_limit_bytes=56 * 2**20)

    def close(*values):
        return [pltpu.with_memory_space_constraint(v, pltpu.VMEM) for v in values]

    packed, factor = pl.pallas_call(
        functools.partial(pack_kernel, 1.0 / (copies * count - 1)),
        out_shape=(shape((PLANES, ROWS, width), f32), shape((NZ * ROWS, width), f32)),
        in_specs=vmem(7),
        out_specs=tuple(vmem(2)),
    )(*close(increment, kappa_east, kappa_north, kappa_vertical, cell_area, norm_weight, bottom_level))

    fields = pl.pallas_call(
        turn_kernel,
        out_shape=shape((groups, NZ, width, lanes), f32),
        in_specs=vmem(1),
        out_specs=vmem(1)[0],
        compiler_params=params,
    )(perturbations)

    def swap(x, k):
        return lax.ppermute(x, "mem", [(i, i ^ k) for i in range(count)])

    pair = jnp.stack([packed, swap(packed, half)])
    blocks = [pair] + [swap(pair, k) for k in range(1, half)]

    start, coefs, near, far = pl.pallas_call(
        functools.partial(spread_kernel, count, width, copies // groups),
        out_shape=(
            shape((groups, NZ, width, lanes), f32),
            shape((4, width, lanes), f32),
            shape((groups * NZ + 4, HALO, lanes), f32),
            shape((groups * NZ + 4, HALO, lanes), f32),
        ),
        in_specs=vmem(half + 1),
        out_specs=tuple(vmem(4)),
        scratch_shapes=[pltpu.VMEM((PLANES, rows, width), f32)],
        compiler_params=params,
    )(*close(*blocks, fields))

    far = lax.ppermute(far, "tile", [(i, (i - 1 if i % 2 == 0 else i + 1) % sides) for i in range(sides)])
    near = lax.ppermute(near, "tile", [(i, i ^ 1) for i in range(sides)])

    tall = width + 4 * HALO
    state = pltpu.VMEM((groups, NZ, tall, lanes), f32)
    big = pltpu.VMEM((NZ, tall, lanes), f32)
    parts = pl.pallas_call(
        functools.partial(diffuse_kernel, count, rows, sides),
        out_shape=tuple(shape((2, NZ * ROWS, width), f32) for k in range(half)),
        in_specs=vmem(5),
        out_specs=tuple(vmem(half)),
        scratch_shapes=[state] * 2
        + [big] * 2
        + [
            pltpu.VMEM((4, tall, lanes), f32),
            pltpu.VMEM((9, tall, lanes), f32),
            pltpu.VMEM((groups, NZ, width, lanes), f32),
            pltpu.VMEM((NZ, rows, width), f32),
        ],
        compiler_params=params,
    )(*close(fields, start, coefs, near, far))

    pieces = [parts[0]] + [swap(parts[k], k) for k in range(1, half)]
    sent = sum(piece[1] for piece in pieces)
    kept = sum(piece[0] for piece in pieces)
    total = (kept + swap(sent, half)) * factor
    return total.reshape(NZ, ROWS, width)


def solution(mesh):
    flat = P("mem", "tile")
    deep = P(None, "mem", "tile")
    return jax.shard_map(
        local,
        mesh=mesh,
        in_specs=(P("mem", None, None, "tile"), deep, flat, flat, flat, flat, flat, flat),
        out_specs=deep,
        check_vma=False,
    )
```

```python
import functools

import jax
import jax.numpy as jnp
from jax import lax
from jax.experimental import pallas as pl
from jax.experimental.pallas import tpu as pltpu
from jax.sharding import PartitionSpec as P

NZ = 12
STEPS = 4
HALO = 2 * STEPS
PLANES = NZ + 4
ROWS = 8
UNROLL = 9


def vmem(count):
    return [pl.BlockSpec(memory_space=pltpu.VMEM)] * count


def pack_kernel(share, inc, east, north, up, area, norm, bottom, out, factor):
    levels = bottom[...].astype(jnp.float32)
    weight = norm[...]
    for z in range(NZ):
        out[z] = jnp.where(levels > z, weight * inc[z], 0.0)
        factor[z * ROWS : (z + 1) * ROWS] = jnp.where(levels > z, weight * share, 0.0)
    out[NZ] = east[...]
    out[NZ + 1] = north[...]
    out[NZ + 2] = up[...]
    out[NZ + 3] = area[...] + 4.0 * levels


def unpack(packed):
    levels = jnp.floor(packed * 0.25)
    return jnp.maximum(packed - 4.0 * levels, 1.0), levels


def turn_kernel(members, fields):
    groups = fields.shape[0]
    copies = members.shape[0] // groups
    for g in range(groups):
        for z in range(NZ):
            rows = [members[g * copies + m, z].astype(jnp.float32) for m in range(copies)]
            fields[g, z] = jnp.concatenate(rows, axis=0).T


def spread_kernel(count, width, copies, *refs):
    half = count // 2
    blocks = refs[:half]
    fields, start, coefs, near, far, whole = refs[half:]
    groups = fields.shape[0]
    me = lax.axis_index("mem")
    even = lax.rem(lax.axis_index("tile"), 2) == 0
    for k in range(half):
        for h in range(2):
            row = pl.multiple_of((me ^ (k + h * half)) * ROWS, ROWS)
            for q in range(PLANES):
                whole[q, pl.ds(row, ROWS), :] = blocks[k][h, q]

    def turned(q):
        plane = whole[q]
        return jnp.concatenate([plane] * copies, axis=0).T

    packed = turned(PLANES - 1)
    area, unused = unpack(packed)
    inverse = 1.0 / area

    def edges(q, value):
        low, high = value[:HALO], value[width - HALO :]
        near[q] = jnp.where(even, high, low)
        far[q] = jnp.where(even, low, high)

    for q in range(4):
        value = packed if q == 3 else turned(NZ + q)
        coefs[q] = value
        edges(groups * NZ + q, value)
    for z in range(NZ):
        scaled = turned(z) * inverse
        for g in range(groups):
            first = fields[g, z] * scaled
            start[g, z] = first
            edges(g * NZ + z, first)


def diffuse_kernel(count, rows, sides, fields, start, coefs, near, far, *refs):
    half = count // 2
    outs = refs[:half]
    ping, pong, east, north, south, flat, plane, final, joined = refs[half:]
    groups, nz, width, lanes = start.shape
    pad = HALO
    me = lax.axis_index("mem")
    tile = lax.axis_index("tile")
    even = lax.rem(tile, 2) == 0
    first_tile = tile == 0
    last_tile = tile == sides - 1

    def left(q):
        return jnp.where(first_tile, 0.0, jnp.where(even, far[q], near[q]))

    def right(q):
        return jnp.where(last_tile, 0.0, jnp.where(even, near[q], far[q]))

    tiles = width // HALO + 2
    total = width + 2 * HALO
    zero = jnp.zeros((pad, lanes), jnp.float32)

    def widen(ref, index, before, inner, after):
        ref[(*index, slice(0, pad))] = zero
        ref[(*index, slice(pad, 2 * pad))] = before
        ref[(*index, slice(2 * pad, 2 * pad + width))] = inner
        ref[(*index, slice(2 * pad + width, 3 * pad + width))] = after
        ref[(*index, slice(pad + total, 2 * pad + total))] = zero

    for g in range(groups):
        for z in range(NZ):
            widen(ping, (g, z), left(g * NZ + z), start[g, z], right(g * NZ + z))
            pong[g, z, 0:pad] = zero
            pong[g, z, pad + total : 2 * pad + total] = zero
    for q in range(4):
        widen(flat, (q,), left(groups * NZ + q), coefs[q], right(groups * NZ + q))
    lane = lax.broadcasted_iota(jnp.int32, (HALO, lanes), 1)
    last = lane % rows == rows - 1

    for z in range(NZ):
        east[z, 0:pad] = zero

    def weights(tile, carry):
        first = pl.multiple_of(pad + tile * HALO, HALO)
        here = pl.ds(first, HALO)
        area, levels = unpack(flat[3, here, :])
        unused, levels_east = unpack(flat[3, pl.ds(first + 1, HALO), :])
        depth = jnp.minimum(levels, levels_east)
        face = flat[0, here, :]
        face_n = jnp.where(last, 0.0, flat[1, here, :])
        face_s = pltpu.roll(face_n, 1, 1)
        depth_n = jnp.minimum(levels, pltpu.roll(levels, lanes - 1, 1))
        depth_s = pltpu.roll(depth_n, 1, 1)
        for z in range(NZ):
            east[z, here, :] = jnp.where(depth > z, face, 0.0)
            north[z, here, :] = jnp.where(depth_n > z, face_n, 0.0)
            south[z, here, :] = jnp.where(depth_s > z, face_s, 0.0)
        plane[0, here, :] = jnp.where(last, 0.0, flat[1, here, :])
        plane[1, here, :] = jnp.minimum(levels, pltpu.roll(levels, lanes - 1, 1))
        plane[2, here, :] = levels
        plane[3, here, :] = area
        plane[4, here, :] = 1.0 / area
        return carry

    lax.fori_loop(0, tiles, weights, 0)

    def step(source, target, turn):
        def body(g, tile):
            first = pl.multiple_of(pad + tile * HALO, HALO)
            here = pl.ds(first, HALO)
            levels, area, inverse = [plane[q, here, :] for q in range(2, 5)]
            up = flat[2, here, :]
            centre = source[g, 0, here, :]
            below = None
            for z in range(NZ):
                total = east[z, here, :] * (source[g, z, pl.ds(first + 1, HALO), :] - centre)
                total -= east[z, pl.ds(first - 1, HALO), :] * (centre - source[g, z, pl.ds(first - 1, HALO), :])
                flux = north[z, here, :] * (pltpu.roll(centre, lanes - 1, 1) - centre)
                total += flux
                total -= south[z, here, :] * (centre - pltpu.roll(centre, 1, 1))
                if z > 0:
                    total -= below
                now = centre
                if z < NZ - 1:
                    centre = source[g, z + 1, here, :]
                    below = jnp.where(levels > z + 1, up, 0.0) * (centre - now)
                    total += below
                if turn == STEPS - 1:
                    total = now * area + total
                else:
                    total = now + total * inverse
                if turn == 2 * STEPS - 1:
                    inner = pl.ds(pl.multiple_of(tile * HALO - HALO, HALO), HALO)
                    final[g, z, inner, :] = total * fields[g, z, inner, :]
                else:
                    target[g, z, here, :] = total

        edge = 1 if turn == 2 * STEPS - 1 else 0
        for g in range(groups):

            run = max(r for r in range(1, UNROLL + 1) if (tiles - 2 * edge) % r == 0)

            @pl.loop(0, (tiles - 2 * edge) // run)
            def sweep(turn_of):
                for k in range(run):
                    body(g, edge + turn_of * run + k)

    for turn in range(2 * STEPS):
        source, target = (ping, pong) if turn % 2 == 0 else (pong, ping)
        step(source, target, turn)
    for z in range(NZ):
        parts = []
        for g in range(groups):
            turned = final[g, z].T
            parts += [turned[first : first + rows] for first in range(0, lanes, rows)]
        summed = parts[0]
        for part in parts[1:]:
            summed = summed + part
        joined[z] = summed
    for k in range(half):
        for h in range(2):
            row = pl.multiple_of((me ^ (k + h * half)) * ROWS, ROWS)
            for z in range(NZ):
                outs[k][h, z * ROWS : (z + 1) * ROWS, :] = joined[z, pl.ds(row, ROWS), :]


def local(perturbations, increment, kappa_east, kappa_north, kappa_vertical, cell_area, norm_weight, bottom_level):
    count = lax.axis_size("mem")
    sides = lax.axis_size("tile")
    copies, nz, rows, width = perturbations.shape
    lanes = 128
    groups = copies * rows // lanes
    half = count // 2
    f32 = jnp.float32
    shape = pltpu.VMEM
    params = pltpu.CompilerParams(vmem_limit_bytes=56 * 2**20)

    def close(*values):
        return [pltpu.with_memory_space_constraint(v, pltpu.VMEM) for v in values]

    packed, factor = pl.pallas_call(
        functools.partial(pack_kernel, 1.0 / (copies * count - 1)),
        out_shape=(shape((PLANES, ROWS, width), f32), shape((NZ * ROWS, width), f32)),
        in_specs=vmem(7),
        out_specs=tuple(vmem(2)),
    )(increment, kappa_east, kappa_north, kappa_vertical, cell_area, norm_weight, bottom_level)

    fields = pl.pallas_call(
        turn_kernel,
        out_shape=shape((groups, NZ, width, lanes), f32),
        in_specs=vmem(1),
        out_specs=vmem(1)[0],
        compiler_params=params,
    )(perturbations)

    def swap(x, k):
        return lax.ppermute(x, "mem", [(i, i ^ k) for i in range(count)])

    pair = jnp.stack([packed, swap(packed, half)])
    blocks = [pair] + [swap(pair, k) for k in range(1, half)]

    start, coefs, near, far = pl.pallas_call(
        functools.partial(spread_kernel, count, width, copies // groups),
        out_shape=(
            shape((groups, NZ, width, lanes), f32),
            shape((4, width, lanes), f32),
            shape((groups * NZ + 4, HALO, lanes), f32),
            shape((groups * NZ + 4, HALO, lanes), f32),
        ),
        in_specs=vmem(half + 1),
        out_specs=tuple(vmem(4)),
        scratch_shapes=[pltpu.VMEM((PLANES, rows, width), f32)],
        compiler_params=params,
    )(*close(*blocks, fields))

    far = lax.ppermute(far, "tile", [(i, (i - 1 if i % 2 == 0 else i + 1) % sides) for i in range(sides)])
    near = lax.ppermute(near, "tile", [(i, i ^ 1) for i in range(sides)])

    tall = width + 4 * HALO
    state = pltpu.VMEM((groups, NZ, tall, lanes), f32)
    parts = pl.pallas_call(
        functools.partial(diffuse_kernel, count, rows, sides),
        out_shape=tuple(shape((2, NZ * ROWS, width), f32) for k in range(half)),
        in_specs=vmem(5),
        out_specs=tuple(vmem(half)),
        scratch_shapes=[state] * 2
        + [
            pltpu.VMEM((NZ, tall, lanes), f32),
            pltpu.VMEM((NZ, tall, lanes), f32),
            pltpu.VMEM((NZ, tall, lanes), f32),
            pltpu.VMEM((4, tall, lanes), f32),
            pltpu.VMEM((5, tall, lanes), f32),
            pltpu.VMEM((groups, NZ, width, lanes), f32),
            pltpu.VMEM((NZ, rows, width), f32),
        ],
        compiler_params=params,
    )(*close(fields, start, coefs, near, far))

    pieces = [parts[0]] + [swap(parts[k], k) for k in range(1, half)]
    sent = sum(piece[1] for piece in pieces)
    kept = sum(piece[0] for piece in pieces)
    total = (kept + swap(sent, half)) * factor
    return total.reshape(NZ, ROWS, width)


def solution(mesh):
    flat = P("mem", "tile")
    deep = P(None, "mem", "tile")
    return jax.shard_map(
        local,
        mesh=mesh,
        in_specs=(P("mem", None, None, "tile"), deep, flat, flat, flat, flat, flat, flat),
        out_specs=deep,
        check_vma=False,
    )
```

```python
import functools

import jax
import jax.numpy as jnp
from jax import lax
from jax.experimental import pallas as pl
from jax.experimental.pallas import tpu as pltpu
from jax.sharding import PartitionSpec as P

NZ = 12
STEPS = 4
HALO = 2 * STEPS
COEFS = 5
PLANES = NZ + COEFS + 1
FULL = 32000.0
KAPPA = 200000.0
AREA = 32000.0
PER_LOG = 256.0
TINY = 1e-37
ROWS = 8
UNROLL = 9


def vmem(count):
    return [pl.BlockSpec(memory_space=pltpu.VMEM)] * count


def pack_kernel(share, inc, east, north, up, area, norm, bottom, out, factor):
    levels = bottom[...].astype(jnp.float32)
    weight = norm[...]
    lane = lax.broadcasted_iota(jnp.int32, weight.shape, 1)

    def put(q, value):
        out[q] = jnp.round(value).astype(jnp.int32).astype(jnp.int16)

    sizes = jnp.zeros_like(weight)
    for z in range(NZ):
        scaled = jnp.where(levels > z, weight * inc[z], 0.0)
        largest = jnp.maximum(jnp.max(jnp.abs(scaled), axis=1, keepdims=True), TINY)
        size = jnp.ceil(jnp.log(largest) * PER_LOG)
        put(z, scaled * (FULL / jnp.exp(size * (1.0 / PER_LOG))))
        sizes = jnp.where(lane == z, size, sizes)
        factor[z * ROWS : (z + 1) * ROWS] = jnp.where(levels > z, weight * share, 0.0)
    put(NZ, east[...] * KAPPA)
    put(NZ + 1, north[...] * KAPPA)
    put(NZ + 2, up[...] * KAPPA)
    put(NZ + 3, (area[...] - 1.0) * AREA)
    put(NZ + 4, levels)
    put(NZ + 5, sizes)


def turn_kernel(members, fields):
    groups = fields.shape[0]
    copies = members.shape[0] // groups
    for g in range(groups):
        for z in range(NZ):
            rows = [members[g * copies + m, z].astype(jnp.float32) for m in range(copies)]
            fields[g, z] = jnp.concatenate(rows, axis=0).T


def spread_kernel(count, width, copies, *refs):
    half = count // 2
    blocks = refs[:half]
    fields, start, coefs, near, far, whole = refs[half:]
    groups = fields.shape[0]
    me = lax.axis_index("mem")
    even = lax.rem(lax.axis_index("tile"), 2) == 0
    for k in range(half):
        for h in range(2):
            row = pl.multiple_of((me ^ (k + h * half)) * ROWS, ROWS)
            for q in range(PLANES):
                whole[q, pl.ds(row, ROWS), :] = blocks[k][h, q].astype(jnp.int32).astype(jnp.float32)

    def turned(q):
        plane = whole[q]
        return jnp.concatenate([plane] * copies, axis=0).T

    sizes = jnp.exp(turned(PLANES - 1)[0 : 2 * ROWS] * (1.0 / PER_LOG)) * (1.0 / FULL)
    area = turned(NZ + 3) * (1.0 / AREA) + 1.0
    inverse = 1.0 / area

    def edges(q, value):
        low, high = value[:HALO], value[width - HALO :]
        near[q] = jnp.where(even, high, low)
        far[q] = jnp.where(even, low, high)

    for q in range(COEFS):
        value = turned(NZ + q) * (1.0 / KAPPA) if q < 3 else area if q == 3 else turned(NZ + q)
        coefs[q] = value
        edges(groups * NZ + q, value)
    for z in range(NZ):
        scaled = turned(z) * (inverse * sizes[z : z + 1])
        for g in range(groups):
            first = fields[g, z] * scaled
            start[g, z] = first
            edges(g * NZ + z, first)


def diffuse_kernel(count, rows, sides, fields, start, coefs, near, far, *refs):
    half = count // 2
    outs = refs[:half]
    ping, pong, east, north, south, flat, plane, final, joined = refs[half:]
    groups, nz, width, lanes = start.shape
    pad = HALO
    me = lax.axis_index("mem")
    tile = lax.axis_index("tile")
    even = lax.rem(tile, 2) == 0
    first_tile = tile == 0
    last_tile = tile == sides - 1

    def left(q):
        return jnp.where(first_tile, 0.0, jnp.where(even, far[q], near[q]))

    def right(q):
        return jnp.where(last_tile, 0.0, jnp.where(even, near[q], far[q]))

    tiles = width // HALO + 2
    total = width + 2 * HALO
    zero = jnp.zeros((pad, lanes), jnp.float32)

    def widen(ref, index, before, inner, after):
        ref[(*index, slice(0, pad))] = zero
        ref[(*index, slice(pad, 2 * pad))] = before
        ref[(*index, slice(2 * pad, 2 * pad + width))] = inner
        ref[(*index, slice(2 * pad + width, 3 * pad + width))] = after
        ref[(*index, slice(pad + total, 2 * pad + total))] = zero

    for g in range(groups):
        for z in range(NZ):
            widen(ping, (g, z), left(g * NZ + z), start[g, z], right(g * NZ + z))
            pong[g, z, 0:pad] = zero
            pong[g, z, pad + total : 2 * pad + total] = zero
    for q in range(COEFS):
        widen(flat, (q,), left(groups * NZ + q), coefs[q], right(groups * NZ + q))
    lane = lax.broadcasted_iota(jnp.int32, (HALO, lanes), 1)
    last = lane % rows == rows - 1

    for z in range(NZ):
        east[z, 0:pad] = zero

    def weights(tile, carry):
        first = pl.multiple_of(pad + tile * HALO, HALO)
        here = pl.ds(first, HALO)
        area = jnp.maximum(flat[3, here, :], 1.0)
        levels = flat[4, here, :]
        levels_east = flat[4, pl.ds(first + 1, HALO), :]
        depth = jnp.minimum(levels, levels_east)
        face = flat[0, here, :]
        face_n = jnp.where(last, 0.0, flat[1, here, :])
        face_s = pltpu.roll(face_n, 1, 1)
        depth_n = jnp.minimum(levels, pltpu.roll(levels, lanes - 1, 1))
        depth_s = pltpu.roll(depth_n, 1, 1)
        for z in range(NZ):
            east[z, here, :] = jnp.where(depth > z, face, 0.0)
            north[z, here, :] = jnp.where(depth_n > z, face_n, 0.0)
            south[z, here, :] = jnp.where(depth_s > z, face_s, 0.0)
        plane[0, here, :] = jnp.where(last, 0.0, flat[1, here, :])
        plane[1, here, :] = jnp.minimum(levels, pltpu.roll(levels, lanes - 1, 1))
        plane[2, here, :] = levels
        plane[3, here, :] = area
        plane[4, here, :] = 1.0 / area
        return carry

    lax.fori_loop(0, tiles, weights, 0)

    def step(source, target, turn):
        def body(g, tile):
            first = pl.multiple_of(pad + tile * HALO, HALO)
            here = pl.ds(first, HALO)
            levels, area, inverse = [plane[q, here, :] for q in range(2, 5)]
            up = flat[2, here, :]
            centre = source[g, 0, here, :]
            below = None
            for z in range(NZ):
                total = east[z, here, :] * (source[g, z, pl.ds(first + 1, HALO), :] - centre)
                total -= east[z, pl.ds(first - 1, HALO), :] * (centre - source[g, z, pl.ds(first - 1, HALO), :])
                flux = north[z, here, :] * (pltpu.roll(centre, lanes - 1, 1) - centre)
                total += flux
                total -= south[z, here, :] * (centre - pltpu.roll(centre, 1, 1))
                if z > 0:
                    total -= below
                now = centre
                if z < NZ - 1:
                    centre = source[g, z + 1, here, :]
                    below = jnp.where(levels > z + 1, up, 0.0) * (centre - now)
                    total += below
                if turn == STEPS - 1:
                    total = now * area + total
                else:
                    total = now + total * inverse
                if turn == 2 * STEPS - 1:
                    inner = pl.ds(pl.multiple_of(tile * HALO - HALO, HALO), HALO)
                    final[g, z, inner, :] = total * fields[g, z, inner, :]
                else:
                    target[g, z, here, :] = total

        edge = 1 if turn == 2 * STEPS - 1 else 0
        for g in range(groups):

            run = max(r for r in range(1, UNROLL + 1) if (tiles - 2 * edge) % r == 0)

            @pl.loop(0, (tiles - 2 * edge) // run)
            def sweep(turn_of):
                for k in range(run):
                    body(g, edge + turn_of * run + k)

    for turn in range(2 * STEPS):
        source, target = (ping, pong) if turn % 2 == 0 else (pong, ping)
        step(source, target, turn)
    for z in range(NZ):
        parts = []
        for g in range(groups):
            turned = final[g, z].T
            parts += [turned[first : first + rows] for first in range(0, lanes, rows)]
        summed = parts[0]
        for part in parts[1:]:
            summed = summed + part
        joined[z] = summed
    for k in range(half):
        for h in range(2):
            row = pl.multiple_of((me ^ (k + h * half)) * ROWS, ROWS)
            for z in range(NZ):
                outs[k][h, z * ROWS : (z + 1) * ROWS, :] = joined[z, pl.ds(row, ROWS), :]


def local(perturbations, increment, kappa_east, kappa_north, kappa_vertical, cell_area, norm_weight, bottom_level):
    count = lax.axis_size("mem")
    sides = lax.axis_size("tile")
    copies, nz, rows, width = perturbations.shape
    lanes = 128
    groups = copies * rows // lanes
    half = count // 2
    f32 = jnp.float32
    shape = pltpu.VMEM
    params = pltpu.CompilerParams(vmem_limit_bytes=56 * 2**20)

    def close(*values):
        return [pltpu.with_memory_space_constraint(v, pltpu.VMEM) for v in values]

    packed, factor = pl.pallas_call(
        functools.partial(pack_kernel, 1.0 / (copies * count - 1)),
        out_shape=(shape((PLANES, ROWS, width), jnp.int16), shape((NZ * ROWS, width), f32)),
        in_specs=vmem(7),
        out_specs=tuple(vmem(2)),
    )(increment, kappa_east, kappa_north, kappa_vertical, cell_area, norm_weight, bottom_level)

    fields = pl.pallas_call(
        turn_kernel,
        out_shape=shape((groups, NZ, width, lanes), f32),
        in_specs=vmem(1),
        out_specs=vmem(1)[0],
        compiler_params=params,
    )(perturbations)

    def swap(x, k):
        return lax.ppermute(x, "mem", [(i, i ^ k) for i in range(count)])

    pair = jnp.stack([packed, swap(packed, half)])
    blocks = [pair] + [swap(pair, k) for k in range(1, half)]

    start, coefs, near, far = pl.pallas_call(
        functools.partial(spread_kernel, count, width, copies // groups),
        out_shape=(
            shape((groups, NZ, width, lanes), f32),
            shape((COEFS, width, lanes), f32),
            shape((groups * NZ + COEFS, HALO, lanes), f32),
            shape((groups * NZ + COEFS, HALO, lanes), f32),
        ),
        in_specs=vmem(half + 1),
        out_specs=tuple(vmem(4)),
        scratch_shapes=[pltpu.VMEM((PLANES, rows, width), f32)],
        compiler_params=params,
    )(*close(*blocks, fields))

    far = lax.ppermute(far, "tile", [(i, (i - 1 if i % 2 == 0 else i + 1) % sides) for i in range(sides)])
    near = lax.ppermute(near, "tile", [(i, i ^ 1) for i in range(sides)])

    tall = width + 4 * HALO
    state = pltpu.VMEM((groups, NZ, tall, lanes), f32)
    parts = pl.pallas_call(
        functools.partial(diffuse_kernel, count, rows, sides),
        out_shape=tuple(shape((2, NZ * ROWS, width), f32) for k in range(half)),
        in_specs=vmem(5),
        out_specs=tuple(vmem(half)),
        scratch_shapes=[state] * 2
        + [
            pltpu.VMEM((NZ, tall, lanes), f32),
            pltpu.VMEM((NZ, tall, lanes), f32),
            pltpu.VMEM((NZ, tall, lanes), f32),
            pltpu.VMEM((COEFS, tall, lanes), f32),
            pltpu.VMEM((5, tall, lanes), f32),
            pltpu.VMEM((groups, NZ, width, lanes), f32),
            pltpu.VMEM((NZ, rows, width), f32),
        ],
        compiler_params=params,
    )(*close(fields, start, coefs, near, far))

    pieces = [parts[0]] + [swap(parts[k], k) for k in range(1, half)]
    sent = sum(piece[1] for piece in pieces)
    kept = sum(piece[0] for piece in pieces)
    total = (kept + swap(sent, half)) * factor
    return total.reshape(NZ, ROWS, width)


def solution(mesh):
    flat = P("mem", "tile")
    deep = P(None, "mem", "tile")
    return jax.shard_map(
        local,
        mesh=mesh,
        in_specs=(P("mem", None, None, "tile"), deep, flat, flat, flat, flat, flat, flat),
        out_specs=deep,
        check_vma=False,
    )
```

```python
import functools

import jax
import jax.numpy as jnp
from jax import lax
from jax.experimental import pallas as pl
from jax.experimental.pallas import tpu as pltpu
from jax.sharding import PartitionSpec as P

NZ = 12
STEPS = 4
HALO = 2 * STEPS
COEFS = 5
PLANES = NZ + COEFS + 1
FULL = 32000.0
KAPPA = 200000.0
AREA = 32000.0
PER_LOG = 256.0
TINY = 1e-37
ROWS = 8
UNROLL = 9
WORK = 7
EARLY = 2


def vmem(count):
    return [pl.BlockSpec(memory_space=pltpu.VMEM)] * count


def pack_kernel(share, inc, east, north, up, area, norm, bottom, out, factor):
    levels = bottom[...].astype(jnp.float32)
    weight = norm[...]
    lane = lax.broadcasted_iota(jnp.int32, weight.shape, 1)

    def put(q, value):
        out[q] = jnp.round(value).astype(jnp.int32).astype(jnp.int16)

    sizes = jnp.zeros_like(weight)
    for z in range(NZ):
        scaled = jnp.where(levels > z, weight * inc[z], 0.0)
        largest = jnp.maximum(jnp.max(jnp.abs(scaled), axis=1, keepdims=True), TINY)
        size = jnp.ceil(jnp.log(largest) * PER_LOG)
        put(z, scaled * (FULL / jnp.exp(size * (1.0 / PER_LOG))))
        sizes = jnp.where(lane == z, size, sizes)
        factor[z * ROWS : (z + 1) * ROWS] = jnp.where(levels > z, weight * share, 0.0)
    put(NZ, east[...] * KAPPA)
    put(NZ + 1, north[...] * KAPPA)
    put(NZ + 2, up[...] * KAPPA)
    put(NZ + 3, (area[...] - 1.0) * AREA)
    put(NZ + 4, levels)
    put(NZ + 5, sizes)


def turn_kernel(members, fields):
    groups = fields.shape[0]
    copies = members.shape[0] // groups
    for g in range(groups):
        for z in range(NZ):
            rows = [members[g * copies + m, z].astype(jnp.float32) for m in range(copies)]
            fields[g, z] = jnp.concatenate(rows, axis=0).T


def spread_kernel(count, width, copies, *refs):
    half = count // 2
    blocks = refs[:half]
    fields, start, coefs, near, far, whole = refs[half:]
    groups = fields.shape[0]
    me = lax.axis_index("mem")
    even = lax.rem(lax.axis_index("tile"), 2) == 0
    for k in range(half):
        for h in range(2):
            row = pl.multiple_of((me ^ (k + h * half)) * ROWS, ROWS)
            for q in range(PLANES):
                whole[q, pl.ds(row, ROWS), :] = blocks[k][h, q].astype(jnp.int32).astype(jnp.float32)

    def turned(q):
        plane = whole[q]
        return jnp.concatenate([plane] * copies, axis=0).T

    sizes = jnp.exp(turned(PLANES - 1)[0 : 2 * ROWS] * (1.0 / PER_LOG)) * (1.0 / FULL)
    area = turned(NZ + 3) * (1.0 / AREA) + 1.0
    inverse = 1.0 / area

    def edges(q, value):
        low, high = value[:HALO], value[width - HALO :]
        near[q] = jnp.where(even, high, low)
        far[q] = jnp.where(even, low, high)

    for q in range(COEFS):
        value = turned(NZ + q) * (1.0 / KAPPA) if q < 3 else area if q == 3 else turned(NZ + q)
        coefs[q] = value
        edges(groups * NZ + q, value)
    for z in range(NZ):
        scaled = turned(z) * (inverse * sizes[z : z + 1])
        for g in range(groups):
            first = fields[g, z] * scaled
            start[g, z] = first
            edges(g * NZ + z, first)


class Sweep:
    def __init__(self, rows, work):
        self.ping, self.pong, self.east, self.north, self.south, self.flat, self.plane = work
        self.groups, nz, tall, self.lanes = self.ping.shape
        self.tiles = tall // HALO - 2
        lane = lax.broadcasted_iota(jnp.int32, (HALO, self.lanes), 1)
        self.last = lane % rows == rows - 1

    def rows_of(self, tile):
        first = (tile + 1) * HALO
        return first if isinstance(first, int) else pl.multiple_of(first, HALO)

    def weights(self, tile):
        first = self.rows_of(tile)
        here = pl.ds(first, HALO)
        flat, plane = self.flat, self.plane
        area = jnp.maximum(flat[3, here, :], 1.0)
        levels = flat[4, here, :]
        depth = jnp.minimum(levels, flat[4, pl.ds(first + 1, HALO), :])
        face = flat[0, here, :]
        face_n = jnp.where(self.last, 0.0, flat[1, here, :])
        face_s = pltpu.roll(face_n, 1, 1)
        depth_n = jnp.minimum(levels, pltpu.roll(levels, self.lanes - 1, 1))
        depth_s = pltpu.roll(depth_n, 1, 1)
        for z in range(NZ):
            self.east[z, here, :] = jnp.where(depth > z, face, 0.0)
            self.north[z, here, :] = jnp.where(depth_n > z, face_n, 0.0)
            self.south[z, here, :] = jnp.where(depth_s > z, face_s, 0.0)
        plane[0, here, :] = area
        plane[1, here, :] = 1.0 / area

    def step(self, turn, g, tile, give=None):
        source, target = (self.ping, self.pong) if turn % 2 == 0 else (self.pong, self.ping)
        first = self.rows_of(tile)
        here, right, left = pl.ds(first, HALO), pl.ds(first + 1, HALO), pl.ds(first - 1, HALO)
        area, inverse = self.plane[0, here, :], self.plane[1, here, :]
        levels, up = self.flat[4, here, :], self.flat[2, here, :]
        east, north, south, lanes = self.east, self.north, self.south, self.lanes
        centre = source[g, 0, here, :]
        below = None
        for z in range(NZ):
            total = east[z, here, :] * (source[g, z, right, :] - centre)
            total -= east[z, left, :] * (centre - source[g, z, left, :])
            total += north[z, here, :] * (pltpu.roll(centre, lanes - 1, 1) - centre)
            total -= south[z, here, :] * (centre - pltpu.roll(centre, 1, 1))
            if z > 0:
                total -= below
            now = centre
            if z < NZ - 1:
                centre = source[g, z + 1, here, :]
                below = jnp.where(levels > z + 1, up, 0.0) * (centre - now)
                total += below
            total = now * area + total if turn == STEPS - 1 else now + total * inverse
            if give is None:
                target[g, z, here, :] = total
            else:
                give(g, z, tile, total)

    def over(self, turn, begin, end, give=None):
        run = max(r for r in range(1, UNROLL + 1) if (end - begin) % r == 0)
        for g in range(self.groups):

            @pl.loop(0, (end - begin) // run)
            def sweep(block):
                for k in range(run):
                    self.step(turn, g, begin + block * run + k, give)


def begin_kernel(rows, start, coefs, *work):
    state = Sweep(rows, work)
    width = start.shape[2]
    inner = slice(2 * HALO, 2 * HALO + width)
    zero = jnp.zeros((HALO, state.lanes), jnp.float32)
    for z in range(NZ):
        for g in range(state.groups):
            state.ping[g, z, inner] = start[g, z]
            for ref in (state.ping, state.pong):
                ref[g, z, 0:HALO] = zero
                ref[g, z, width + 3 * HALO : width + 4 * HALO] = zero
        state.east[z, 0:HALO] = zero
    for q in range(COEFS):
        state.flat[q, inner] = coefs[q]
        state.flat[q, width + 3 * HALO : width + 4 * HALO] = zero

    @pl.loop(1, state.tiles - 2)
    def fill(tile):
        state.weights(tile)

    for turn in range(EARLY):
        state.over(turn, 2 + turn, state.tiles - 2 - turn)


def diffuse_kernel(count, rows, sides, fields, near, far, *refs):
    half = count // 2
    outs = refs[WORK : WORK + half]
    state = Sweep(rows, refs[WORK + half : 2 * WORK + half])
    final, joined = refs[2 * WORK + half :]
    groups, tiles, lanes = state.groups, state.tiles, state.lanes
    me = lax.axis_index("mem")
    tile = lax.axis_index("tile")
    even = lax.rem(tile, 2) == 0
    first_tile = tile == 0
    last_tile = tile == sides - 1
    low = slice(HALO, 2 * HALO)
    high = slice(tiles * HALO, (tiles + 1) * HALO)

    def edges(ref, index, q):
        ref[(*index, low)] = jnp.where(first_tile, 0.0, jnp.where(even, far[q], near[q]))
        ref[(*index, high)] = jnp.where(last_tile, 0.0, jnp.where(even, near[q], far[q]))

    for q in range(COEFS):
        edges(state.flat, (q,), groups * NZ + q)
    for g in range(groups):
        for z in range(NZ):
            edges(state.ping, (g, z), g * NZ + z)
    for k in (0, tiles - 2, tiles - 1):
        state.weights(k)
    for turn in range(EARLY):
        for g in range(groups):
            for k in range(2 + turn):
                state.step(turn, g, k)
                state.step(turn, g, tiles - 1 - k)
    for turn in range(EARLY, 2 * STEPS - 1):
        state.over(turn, 0, tiles)

    def give(g, z, tile, total):
        inner = pl.ds(pl.multiple_of(tile * HALO - HALO, HALO), HALO)
        final[g, z, inner, :] = total * fields[g, z, inner, :]

    state.over(2 * STEPS - 1, 1, tiles - 1, give)
    for z in range(NZ):
        parts = []
        for g in range(groups):
            turned = final[g, z].T
            parts += [turned[first : first + rows] for first in range(0, lanes, rows)]
        summed = parts[0]
        for part in parts[1:]:
            summed = summed + part
        joined[z] = summed
    for k in range(half):
        for h in range(2):
            row = pl.multiple_of((me ^ (k + h * half)) * ROWS, ROWS)
            for z in range(NZ):
                outs[k][h, z * ROWS : (z + 1) * ROWS, :] = joined[z, pl.ds(row, ROWS), :]


def local(perturbations, increment, kappa_east, kappa_north, kappa_vertical, cell_area, norm_weight, bottom_level):
    count = lax.axis_size("mem")
    sides = lax.axis_size("tile")
    copies, nz, rows, width = perturbations.shape
    lanes = 128
    groups = copies * rows // lanes
    half = count // 2
    f32 = jnp.float32
    shape = pltpu.VMEM
    params = pltpu.CompilerParams(vmem_limit_bytes=32 * 2**20)

    def close(*values):
        return [pltpu.with_memory_space_constraint(v, pltpu.VMEM) for v in values]

    packed, factor = pl.pallas_call(
        functools.partial(pack_kernel, 1.0 / (copies * count - 1)),
        out_shape=(shape((PLANES, ROWS, width), jnp.int16), shape((NZ * ROWS, width), f32)),
        in_specs=vmem(7),
        out_specs=tuple(vmem(2)),
    )(increment, kappa_east, kappa_north, kappa_vertical, cell_area, norm_weight, bottom_level)

    fields = pl.pallas_call(
        turn_kernel,
        out_shape=shape((groups, NZ, width, lanes), f32),
        in_specs=vmem(1),
        out_specs=vmem(1)[0],
        compiler_params=params,
    )(perturbations)

    def swap(x, k):
        return lax.ppermute(x, "mem", [(i, i ^ k) for i in range(count)])

    pair = jnp.stack([packed, swap(packed, half)])
    blocks = [pair] + [swap(pair, k) for k in range(1, half)]

    start, coefs, near, far = pl.pallas_call(
        functools.partial(spread_kernel, count, width, copies // groups),
        out_shape=(
            shape((groups, NZ, width, lanes), f32),
            shape((COEFS, width, lanes), f32),
            shape((groups * NZ + COEFS, HALO, lanes), f32),
            shape((groups * NZ + COEFS, HALO, lanes), f32),
        ),
        in_specs=vmem(half + 1),
        out_specs=tuple(vmem(4)),
        scratch_shapes=[pltpu.VMEM((PLANES, rows, width), f32)],
        compiler_params=params,
    )(*close(*blocks, fields))

    far = lax.ppermute(far, "tile", [(i, (i - 1 if i % 2 == 0 else i + 1) % sides) for i in range(sides)])
    near = lax.ppermute(near, "tile", [(i, i ^ 1) for i in range(sides)])

    tall = width + 4 * HALO
    state = shape((groups, NZ, tall, lanes), f32)
    faces = shape((NZ, tall, lanes), f32)
    work = (state, state, faces, faces, faces, shape((COEFS, tall, lanes), f32), shape((2, tall, lanes), f32))
    begun = pl.pallas_call(
        functools.partial(begin_kernel, rows),
        out_shape=work,
        in_specs=vmem(2),
        out_specs=tuple(vmem(WORK)),
        compiler_params=params,
    )(*close(start, coefs))
    ended = pl.pallas_call(
        functools.partial(diffuse_kernel, count, rows, sides),
        out_shape=tuple(shape((2, NZ * ROWS, width), f32) for k in range(half)) + work,
        in_specs=vmem(3 + WORK),
        out_specs=tuple(vmem(half + WORK)),
        scratch_shapes=[pltpu.VMEM((groups, NZ, width, lanes), f32), pltpu.VMEM((NZ, rows, width), f32)],
        input_output_aliases={3 + k: half + k for k in range(WORK)},
        compiler_params=params,
    )(*close(fields, near, far, *begun))
    parts = ended[:half]

    pieces = [parts[0]] + [swap(parts[k], k) for k in range(1, half)]
    sent = sum(piece[1] for piece in pieces)
    kept = sum(piece[0] for piece in pieces)
    total = (kept + swap(sent, half)) * factor
    return total.reshape(NZ, ROWS, width)


def solution(mesh):
    flat = P("mem", "tile")
    deep = P(None, "mem", "tile")
    return jax.shard_map(
        local,
        mesh=mesh,
        in_specs=(P("mem", None, None, "tile"), deep, flat, flat, flat, flat, flat, flat),
        out_specs=deep,
        check_vma=False,
    )
```

```python
import functools

import jax
import jax.numpy as jnp
from jax import lax
from jax.experimental import pallas as pl
from jax.experimental.pallas import tpu as pltpu
from jax.sharding import PartitionSpec as P

NZ = 12
STEPS = 4
HALO = 2 * STEPS
COEFS = 5
PLANES = NZ + COEFS + 1
FULL = 32000.0
KAPPA = 200000.0
AREA = 32000.0
PER_LOG = 256.0
TINY = 1e-37
ROWS = 8
UNROLL = 9
WORK = 7
EARLY = 1


def vmem(count):
    return [pl.BlockSpec(memory_space=pltpu.VMEM)] * count


def pack_kernel(share, inc, east, north, up, area, norm, bottom, out, factor):
    levels = bottom[...].astype(jnp.float32)
    weight = norm[...]
    lane = lax.broadcasted_iota(jnp.int32, weight.shape, 1)

    def put(q, value):
        out[q] = jnp.round(value).astype(jnp.int32).astype(jnp.int16)

    sizes = jnp.zeros_like(weight)
    for z in range(NZ):
        scaled = jnp.where(levels > z, weight * inc[z], 0.0)
        largest = jnp.maximum(jnp.max(jnp.abs(scaled), axis=1, keepdims=True), TINY)
        size = jnp.ceil(jnp.log(largest) * PER_LOG)
        put(z, scaled * (FULL / jnp.exp(size * (1.0 / PER_LOG))))
        sizes = jnp.where(lane == z, size, sizes)
        factor[z * ROWS : (z + 1) * ROWS] = jnp.where(levels > z, weight * share, 0.0)
    put(NZ, east[...] * KAPPA)
    put(NZ + 1, north[...] * KAPPA)
    put(NZ + 2, up[...] * KAPPA)
    put(NZ + 3, (area[...] - 1.0) * AREA)
    put(NZ + 4, levels)
    put(NZ + 5, sizes)


def turn_kernel(members, fields):
    groups = fields.shape[0]
    copies = members.shape[0] // groups
    for g in range(groups):
        for z in range(NZ):
            rows = [members[g * copies + m, z].astype(jnp.float32) for m in range(copies)]
            fields[g, z] = jnp.concatenate(rows, axis=0).T


def spread_kernel(count, width, copies, *refs):
    half = count // 2
    blocks = refs[:half]
    fields, start, coefs, near, far, whole = refs[half:]
    groups = fields.shape[0]
    me = lax.axis_index("mem")
    even = lax.rem(lax.axis_index("tile"), 2) == 0
    for k in range(half):
        for h in range(2):
            row = pl.multiple_of((me ^ (k + h * half)) * ROWS, ROWS)
            for q in range(PLANES):
                whole[q, pl.ds(row, ROWS), :] = blocks[k][h, q].astype(jnp.int32).astype(jnp.float32)

    def turned(q):
        plane = whole[q]
        return jnp.concatenate([plane] * copies, axis=0).T

    sizes = jnp.exp(turned(PLANES - 1)[0 : 2 * ROWS] * (1.0 / PER_LOG)) * (1.0 / FULL)
    area = turned(NZ + 3) * (1.0 / AREA) + 1.0
    inverse = 1.0 / area

    def edges(q, value):
        low, high = value[:HALO], value[width - HALO :]
        near[q] = jnp.where(even, high, low)
        far[q] = jnp.where(even, low, high)

    for q in range(COEFS):
        value = turned(NZ + q) * (1.0 / KAPPA) if q < 3 else area if q == 3 else turned(NZ + q)
        coefs[q] = value
        edges(groups * NZ + q, value)
    for z in range(NZ):
        scaled = turned(z) * (inverse * sizes[z : z + 1])
        for g in range(groups):
            first = fields[g, z] * scaled
            start[g, z] = first
            edges(g * NZ + z, first)


class Sweep:
    def __init__(self, rows, work):
        self.ping, self.pong, self.east, self.north, self.south, self.flat, self.plane = work
        self.groups, nz, tall, self.lanes = self.ping.shape
        self.tiles = tall // HALO - 2
        lane = lax.broadcasted_iota(jnp.int32, (HALO, self.lanes), 1)
        self.last = lane % rows == rows - 1

    def rows_of(self, tile):
        first = (tile + 1) * HALO
        return first if isinstance(first, int) else pl.multiple_of(first, HALO)

    def weights(self, tile):
        first = self.rows_of(tile)
        here = pl.ds(first, HALO)
        flat, plane = self.flat, self.plane
        area = jnp.maximum(flat[3, here, :], 1.0)
        levels = flat[4, here, :]
        depth = jnp.minimum(levels, flat[4, pl.ds(first + 1, HALO), :])
        face = flat[0, here, :]
        face_n = jnp.where(self.last, 0.0, flat[1, here, :])
        face_s = pltpu.roll(face_n, 1, 1)
        depth_n = jnp.minimum(levels, pltpu.roll(levels, self.lanes - 1, 1))
        depth_s = pltpu.roll(depth_n, 1, 1)
        for z in range(NZ):
            self.east[z, here, :] = jnp.where(depth > z, face, 0.0)
            self.north[z, here, :] = jnp.where(depth_n > z, face_n, 0.0)
            self.south[z, here, :] = jnp.where(depth_s > z, face_s, 0.0)
        plane[0, here, :] = area
        plane[1, here, :] = 1.0 / area

    def step(self, turn, g, tile, give=None):
        source, target = (self.ping, self.pong) if turn % 2 == 0 else (self.pong, self.ping)
        first = self.rows_of(tile)
        here, right, left = pl.ds(first, HALO), pl.ds(first + 1, HALO), pl.ds(first - 1, HALO)
        area, inverse = self.plane[0, here, :], self.plane[1, here, :]
        levels, up = self.flat[4, here, :], self.flat[2, here, :]
        east, north, south, lanes = self.east, self.north, self.south, self.lanes
        centre = source[g, 0, here, :]
        below = None
        for z in range(NZ):
            across = north[z, here, :] * (pltpu.roll(centre, lanes - 1, 1) - centre)
            across += south[z, here, :] * (pltpu.roll(centre, 1, 1) - centre)
            total = east[z, here, :] * (source[g, z, right, :] - centre)
            total += east[z, left, :] * (source[g, z, left, :] - centre)
            if z > 0:
                total -= below
            now = centre
            if z < NZ - 1:
                centre = source[g, z + 1, here, :]
                below = jnp.where(levels > z + 1, up, 0.0) * (centre - now)
                total += below
            total += across
            total = now * area + total if turn == STEPS - 1 else now + total * inverse
            if give is None:
                target[g, z, here, :] = total
            else:
                give(g, z, tile, total)

    def over(self, turn, begin, end, give=None):
        run = max(r for r in range(1, UNROLL + 1) if (end - begin) % r == 0)
        for g in range(self.groups):

            @pl.loop(0, (end - begin) // run)
            def sweep(block):
                for k in range(run):
                    self.step(turn, g, begin + block * run + k, give)


def begin_kernel(rows, start, coefs, *work):
    state = Sweep(rows, work)
    width = start.shape[2]
    inner = slice(2 * HALO, 2 * HALO + width)
    zero = jnp.zeros((HALO, state.lanes), jnp.float32)
    for z in range(NZ):
        for g in range(state.groups):
            state.ping[g, z, inner] = start[g, z]
            for ref in (state.ping, state.pong):
                ref[g, z, 0:HALO] = zero
                ref[g, z, width + 3 * HALO : width + 4 * HALO] = zero
        state.east[z, 0:HALO] = zero
    for q in range(COEFS):
        state.flat[q, inner] = coefs[q]
        state.flat[q, width + 3 * HALO : width + 4 * HALO] = zero

    @pl.loop(1, state.tiles - 2)
    def fill(tile):
        state.weights(tile)

    for turn in range(EARLY):
        state.over(turn, 2 + turn, state.tiles - 2 - turn)


def diffuse_kernel(count, rows, sides, fields, near, far, *refs):
    half = count // 2
    outs = refs[WORK : WORK + half]
    state = Sweep(rows, refs[WORK + half : 2 * WORK + half])
    final, joined = refs[2 * WORK + half :]
    groups, tiles, lanes = state.groups, state.tiles, state.lanes
    me = lax.axis_index("mem")
    tile = lax.axis_index("tile")
    even = lax.rem(tile, 2) == 0
    first_tile = tile == 0
    last_tile = tile == sides - 1
    low = slice(HALO, 2 * HALO)
    high = slice(tiles * HALO, (tiles + 1) * HALO)

    def edges(ref, index, q):
        ref[(*index, low)] = jnp.where(first_tile, 0.0, jnp.where(even, far[q], near[q]))
        ref[(*index, high)] = jnp.where(last_tile, 0.0, jnp.where(even, near[q], far[q]))

    for q in range(COEFS):
        edges(state.flat, (q,), groups * NZ + q)
    for g in range(groups):
        for z in range(NZ):
            edges(state.ping, (g, z), g * NZ + z)
    for k in (0, tiles - 2, tiles - 1):
        state.weights(k)
    for turn in range(EARLY):
        for g in range(groups):
            for k in range(2 + turn):
                state.step(turn, g, k)
                state.step(turn, g, tiles - 1 - k)
    for turn in range(EARLY, 2 * STEPS - 1):
        state.over(turn, 0, tiles)

    def give(g, z, tile, total):
        inner = pl.ds(pl.multiple_of(tile * HALO - HALO, HALO), HALO)
        final[g, z, inner, :] = total * fields[g, z, inner, :]

    state.over(2 * STEPS - 1, 1, tiles - 1, give)
    for z in range(NZ):
        parts = []
        for g in range(groups):
            turned = final[g, z].T
            parts += [turned[first : first + rows] for first in range(0, lanes, rows)]
        summed = parts[0]
        for part in parts[1:]:
            summed = summed + part
        joined[z] = summed
    for k in range(half):
        for h in range(2):
            row = pl.multiple_of((me ^ (k + h * half)) * ROWS, ROWS)
            for z in range(NZ):
                outs[k][h, z * ROWS : (z + 1) * ROWS, :] = joined[z, pl.ds(row, ROWS), :]


def local(perturbations, increment, kappa_east, kappa_north, kappa_vertical, cell_area, norm_weight, bottom_level):
    count = lax.axis_size("mem")
    sides = lax.axis_size("tile")
    copies, nz, rows, width = perturbations.shape
    lanes = 128
    groups = copies * rows // lanes
    half = count // 2
    f32 = jnp.float32
    shape = pltpu.VMEM
    params = pltpu.CompilerParams(vmem_limit_bytes=32 * 2**20)

    def close(*values):
        return [pltpu.with_memory_space_constraint(v, pltpu.VMEM) for v in values]

    packed, factor = pl.pallas_call(
        functools.partial(pack_kernel, 1.0 / (copies * count - 1)),
        out_shape=(shape((PLANES, ROWS, width), jnp.int16), shape((NZ * ROWS, width), f32)),
        in_specs=vmem(7),
        out_specs=tuple(vmem(2)),
    )(increment, kappa_east, kappa_north, kappa_vertical, cell_area, norm_weight, bottom_level)

    fields = pl.pallas_call(
        turn_kernel,
        out_shape=shape((groups, NZ, width, lanes), f32),
        in_specs=vmem(1),
        out_specs=vmem(1)[0],
        compiler_params=params,
    )(perturbations)

    def swap(x, k):
        return lax.ppermute(x, "mem", [(i, i ^ k) for i in range(count)])

    pair = jnp.stack([packed, swap(packed, half)])
    blocks = [pair] + [swap(pair, k) for k in range(1, half)]

    start, coefs, near, far = pl.pallas_call(
        functools.partial(spread_kernel, count, width, copies // groups),
        out_shape=(
            shape((groups, NZ, width, lanes), f32),
            shape((COEFS, width, lanes), f32),
            shape((groups * NZ + COEFS, HALO, lanes), f32),
            shape((groups * NZ + COEFS, HALO, lanes), f32),
        ),
        in_specs=vmem(half + 1),
        out_specs=tuple(vmem(4)),
        scratch_shapes=[pltpu.VMEM((PLANES, rows, width), f32)],
        compiler_params=params,
    )(*close(*blocks, fields))

    far = lax.ppermute(far, "tile", [(i, (i - 1 if i % 2 == 0 else i + 1) % sides) for i in range(sides)])
    near = lax.ppermute(near, "tile", [(i, i ^ 1) for i in range(sides)])

    tall = width + 4 * HALO
    state = shape((groups, NZ, tall, lanes), f32)
    faces = shape((NZ, tall, lanes), f32)
    work = (state, state, faces, faces, faces, shape((COEFS, tall, lanes), f32), shape((2, tall, lanes), f32))
    begun = pl.pallas_call(
        functools.partial(begin_kernel, rows),
        out_shape=work,
        in_specs=vmem(2),
        out_specs=tuple(vmem(WORK)),
        compiler_params=params,
    )(*close(start, coefs))
    ended = pl.pallas_call(
        functools.partial(diffuse_kernel, count, rows, sides),
        out_shape=tuple(shape((2, NZ * ROWS, width), f32) for k in range(half)) + work,
        in_specs=vmem(3 + WORK),
        out_specs=tuple(vmem(half + WORK)),
        scratch_shapes=[pltpu.VMEM((groups, NZ, width, lanes), f32), pltpu.VMEM((NZ, rows, width), f32)],
        input_output_aliases={3 + k: half + k for k in range(WORK)},
        compiler_params=params,
    )(*close(fields, near, far, *begun))
    parts = ended[:half]

    pieces = [parts[0]] + [swap(parts[k], k) for k in range(1, half)]
    sent = sum(piece[1] for piece in pieces)
    kept = sum(piece[0] for piece in pieces)
    total = (kept + swap(sent, half)) * factor
    return total.reshape(NZ, ROWS, width)


def solution(mesh):
    flat = P("mem", "tile")
    deep = P(None, "mem", "tile")
    return jax.shard_map(
        local,
        mesh=mesh,
        in_specs=(P("mem", None, None, "tile"), deep, flat, flat, flat, flat, flat, flat),
        out_specs=deep,
        check_vma=False,
    )
```

```python
import functools

import jax
import jax.numpy as jnp
from jax import lax
from jax.experimental import pallas as pl
from jax.experimental.pallas import tpu as pltpu
from jax.sharding import PartitionSpec as P


NZ = 12
STEPS = 4
HALO = 2 * STEPS
COEFS = 5
PLANES = NZ + COEFS + 1
FULL = 32000.0
KAPPA = 200000.0
AREA = 32000.0
PER_LOG = 256.0
TINY = 1e-37
ROWS = 8
UNROLL = 9
WORK = 7
EARLY = 2


def vmem(count):
    return [pl.BlockSpec(memory_space=pltpu.VMEM)] * count


def coded(value):
    largest = jnp.maximum(jnp.max(jnp.abs(value), axis=1, keepdims=True), TINY)
    size = jnp.ceil(jnp.log(largest) * PER_LOG)
    return value * (FULL / jnp.exp(size * (1.0 / PER_LOG))), size


def short(value):
    return jnp.round(value).astype(jnp.int32).astype(jnp.int16)


def pack_kernel(share, inc, east, north, up, area, norm, bottom, out, factor):
    levels = bottom[...].astype(jnp.float32)
    weight = norm[...]
    lane = lax.broadcasted_iota(jnp.int32, weight.shape, 1)

    def put(q, value):
        out[q] = short(value)

    sizes = jnp.zeros_like(weight)
    for z in range(NZ):
        scaled = jnp.where(levels > z, weight * inc[z], 0.0)
        value, size = coded(scaled)
        put(z, value)
        sizes = jnp.where(lane == z, size, sizes)
        factor[z * ROWS : (z + 1) * ROWS] = jnp.where(levels > z, weight * share, 0.0)
    put(NZ, east[...] * KAPPA)
    put(NZ + 1, north[...] * KAPPA)
    put(NZ + 2, up[...] * KAPPA)
    put(NZ + 3, (area[...] - 1.0) * AREA)
    put(NZ + 4, levels)
    put(NZ + 5, sizes)


def turn_kernel(members, fields):
    groups = fields.shape[0]
    copies = members.shape[0] // groups
    for g in range(groups):
        for z in range(NZ):
            rows = [members[g * copies + m, z].astype(jnp.float32) for m in range(copies)]
            fields[g, z] = jnp.concatenate(rows, axis=0).T


def spread_kernel(count, width, copies, *refs):
    half = count // 2
    blocks = refs[:half]
    fields, start, coefs, near, far, whole = refs[half:]
    groups = fields.shape[0]
    me = lax.axis_index("mem")
    even = lax.rem(lax.axis_index("tile"), 2) == 0
    for k in range(half):
        for h in range(2):
            row = pl.multiple_of((me ^ (k + h * half)) * ROWS, ROWS)
            for q in range(PLANES):
                whole[q, pl.ds(row, ROWS), :] = blocks[k][h, q].astype(jnp.int32).astype(jnp.float32)

    def turned(q):
        plane = whole[q]
        return jnp.concatenate([plane] * copies, axis=0).T

    sizes = jnp.exp(turned(PLANES - 1)[0 : 2 * ROWS] * (1.0 / PER_LOG)) * (1.0 / FULL)
    area = turned(NZ + 3) * (1.0 / AREA) + 1.0
    inverse = 1.0 / area

    def edges(q, value):
        low, high = value[:HALO], value[width - HALO :]
        near[q] = jnp.where(even, high, low)
        far[q] = jnp.where(even, low, high)

    for q in range(COEFS):
        value = turned(NZ + q) * (1.0 / KAPPA) if q < 3 else area if q == 3 else turned(NZ + q)
        coefs[q] = value
        edges(groups * NZ + q, value)
    for z in range(NZ):
        scaled = turned(z) * (inverse * sizes[z : z + 1])
        for g in range(groups):
            first = fields[g, z] * scaled
            start[g, z] = first
            edges(g * NZ + z, first)


class Sweep:
    def __init__(self, rows, work):
        self.ping, self.pong, self.east, self.north, self.south, self.flat, self.plane = work
        self.groups, nz, tall, self.lanes = self.ping.shape
        self.tiles = tall // HALO - 2
        lane = lax.broadcasted_iota(jnp.int32, (HALO, self.lanes), 1)
        self.last = lane % rows == rows - 1

    def rows_of(self, tile):
        first = (tile + 1) * HALO
        return first if isinstance(first, int) else pl.multiple_of(first, HALO)

    def weights(self, tile):
        first = self.rows_of(tile)
        here = pl.ds(first, HALO)
        flat, plane = self.flat, self.plane
        area = jnp.maximum(flat[3, here, :], 1.0)
        levels = flat[4, here, :]
        depth = jnp.minimum(levels, flat[4, pl.ds(first + 1, HALO), :])
        face = flat[0, here, :]
        face_n = jnp.where(self.last, 0.0, flat[1, here, :])
        face_s = pltpu.roll(face_n, 1, 1)
        depth_n = jnp.minimum(levels, pltpu.roll(levels, self.lanes - 1, 1))
        depth_s = pltpu.roll(depth_n, 1, 1)
        for z in range(NZ):
            self.east[z, here, :] = jnp.where(depth > z, face, 0.0)
            self.north[z, here, :] = jnp.where(depth_n > z, face_n, 0.0)
            self.south[z, here, :] = jnp.where(depth_s > z, face_s, 0.0)
        plane[0, here, :] = area
        plane[1, here, :] = 1.0 / area

    def step(self, turn, g, tile, give=None):
        source, target = (self.ping, self.pong) if turn % 2 == 0 else (self.pong, self.ping)
        first = self.rows_of(tile)
        here, right, left = pl.ds(first, HALO), pl.ds(first + 1, HALO), pl.ds(first - 1, HALO)
        area, inverse = self.plane[0, here, :], self.plane[1, here, :]
        levels, up = self.flat[4, here, :], self.flat[2, here, :]
        east, north, south, lanes = self.east, self.north, self.south, self.lanes
        centre = source[g, 0, here, :]
        below = None
        for z in range(NZ):
            across = north[z, here, :] * (pltpu.roll(centre, lanes - 1, 1) - centre)
            across += south[z, here, :] * (pltpu.roll(centre, 1, 1) - centre)
            total = east[z, here, :] * (source[g, z, right, :] - centre)
            total += east[z, left, :] * (source[g, z, left, :] - centre)
            if z > 0:
                total -= below
            now = centre
            if z < NZ - 1:
                centre = source[g, z + 1, here, :]
                below = jnp.where(levels > z + 1, up, 0.0) * (centre - now)
                total += below
            total += across
            total = now * area + total if turn == STEPS - 1 else now + total * inverse
            if give is None:
                target[g, z, here, :] = total
            else:
                give(g, z, tile, total)

    def over(self, turn, begin, end, give=None):
        run = max(r for r in range(1, UNROLL + 1) if (end - begin) % r == 0)
        for g in range(self.groups):

            @pl.loop(0, (end - begin) // run)
            def sweep(block):
                for k in range(run):
                    self.step(turn, g, begin + block * run + k, give)


def begin_kernel(rows, start, coefs, *work):
    state = Sweep(rows, work)
    width = start.shape[2]
    inner = slice(2 * HALO, 2 * HALO + width)
    zero = jnp.zeros((HALO, state.lanes), jnp.float32)
    for z in range(NZ):
        for g in range(state.groups):
            state.ping[g, z, inner] = start[g, z]
            for ref in (state.ping, state.pong):
                ref[g, z, 0:HALO] = zero
                ref[g, z, width + 3 * HALO : width + 4 * HALO] = zero
        state.east[z, 0:HALO] = zero
    for q in range(COEFS):
        state.flat[q, inner] = coefs[q]
        state.flat[q, width + 3 * HALO : width + 4 * HALO] = zero

    @pl.loop(1, state.tiles - 2)
    def fill(tile):
        state.weights(tile)

    for turn in range(EARLY):
        state.over(turn, 2 + turn, state.tiles - 2 - turn)


def diffuse_kernel(count, rows, sides, fields, near, far, *refs):
    half = count // 2
    outs = refs[WORK : WORK + half]
    state = Sweep(rows, refs[WORK + half : 2 * WORK + half])
    final, joined = refs[2 * WORK + half :]
    groups, tiles, lanes = state.groups, state.tiles, state.lanes
    me = lax.axis_index("mem")
    tile = lax.axis_index("tile")
    even = lax.rem(tile, 2) == 0
    first_tile = tile == 0
    last_tile = tile == sides - 1
    low = slice(HALO, 2 * HALO)
    high = slice(tiles * HALO, (tiles + 1) * HALO)

    def edges(ref, index, q):
        ref[(*index, low)] = jnp.where(first_tile, 0.0, jnp.where(even, far[q], near[q]))
        ref[(*index, high)] = jnp.where(last_tile, 0.0, jnp.where(even, near[q], far[q]))

    for q in range(COEFS):
        edges(state.flat, (q,), groups * NZ + q)
    for g in range(groups):
        for z in range(NZ):
            edges(state.ping, (g, z), g * NZ + z)
    for k in (0, tiles - 2, tiles - 1):
        state.weights(k)
    for turn in range(EARLY):
        for g in range(groups):
            for k in range(2 + turn):
                state.step(turn, g, k)
                state.step(turn, g, tiles - 1 - k)
    for turn in range(EARLY, 2 * STEPS - 1):
        state.over(turn, 0, tiles)

    def give(g, z, tile, total):
        inner = pl.ds(pl.multiple_of(tile * HALO - HALO, HALO), HALO)
        final[g, z, inner, :] = total * fields[g, z, inner, :]

    state.over(2 * STEPS - 1, 1, tiles - 1, give)
    for z in range(NZ):
        parts = []
        for g in range(groups):
            turned = final[g, z].T
            parts += [turned[first : first + rows] for first in range(0, lanes, rows)]
        summed = parts[0]
        for part in parts[1:]:
            summed = summed + part
        joined[z] = summed
    lane = lax.broadcasted_iota(jnp.int32, (ROWS, joined.shape[2]), 1)
    for k in range(half):
        for h in range(2):
            row = pl.multiple_of((me ^ (k + h * half)) * ROWS, ROWS)
            sizes = jnp.zeros(lane.shape, jnp.float32)
            for z in range(NZ):
                value = joined[z, pl.ds(row, ROWS), :]
                if k == 0:
                    outs[k][h, z] = value
                else:
                    value, size = coded(value)
                    outs[k][h, z] = short(value)
                    sizes = jnp.where(lane == z, size, sizes)
            if k > 0:
                outs[k][h, NZ] = short(sizes)


def gather_kernel(half, *refs):
    own, received, (kept, sent) = refs[0], refs[1:half], refs[half:]
    for h, out in enumerate((kept, sent)):
        scales = []
        for part in received:
            sizes = part[h, NZ].astype(jnp.int32).astype(jnp.float32)
            scales.append(jnp.exp(sizes * (1.0 / PER_LOG)) * (1.0 / FULL))
        for z in range(NZ):
            total = own[h, z]
            for part, scale in zip(received, scales):
                total += part[h, z].astype(jnp.int32).astype(jnp.float32) * scale[:, z : z + 1]
            out[z * ROWS : (z + 1) * ROWS] = total


def local(perturbations, increment, kappa_east, kappa_north, kappa_vertical, cell_area, norm_weight, bottom_level):
    count = lax.axis_size("mem")
    sides = lax.axis_size("tile")
    copies, _, rows, width = perturbations.shape
    lanes = 128
    groups = copies * rows // lanes
    half = count // 2
    f32 = jnp.float32
    shape = pltpu.VMEM
    params = pltpu.CompilerParams(vmem_limit_bytes=32 * 2**20)

    def close(*values):
        return [pltpu.with_memory_space_constraint(v, pltpu.VMEM) for v in values]

    packed, factor = pl.pallas_call(
        functools.partial(pack_kernel, 1.0 / (copies * count - 1)),
        out_shape=(shape((PLANES, ROWS, width), jnp.int16), shape((NZ * ROWS, width), f32)),
        in_specs=vmem(7),
        out_specs=tuple(vmem(2)),
    )(increment, kappa_east, kappa_north, kappa_vertical, cell_area, norm_weight, bottom_level)

    fields = pl.pallas_call(
        turn_kernel,
        out_shape=shape((groups, NZ, width, lanes), f32),
        in_specs=vmem(1),
        out_specs=vmem(1)[0],
        compiler_params=params,
    )(perturbations)

    def swap(x, k):
        return lax.ppermute(x, "mem", [(i, i ^ k) for i in range(count)])

    pair = jnp.stack([packed, swap(packed, half)])
    blocks = [pair] + [swap(pair, k) for k in range(1, half)]

    start, coefs, near, far = pl.pallas_call(
        functools.partial(spread_kernel, count, width, copies // groups),
        out_shape=(
            shape((groups, NZ, width, lanes), f32),
            shape((COEFS, width, lanes), f32),
            shape((groups * NZ + COEFS, HALO, lanes), f32),
            shape((groups * NZ + COEFS, HALO, lanes), f32),
        ),
        in_specs=vmem(half + 1),
        out_specs=tuple(vmem(4)),
        scratch_shapes=[pltpu.VMEM((PLANES, rows, width), f32)],
        compiler_params=params,
    )(*close(*blocks, fields))

    far = lax.ppermute(far, "tile", [(i, (i - 1 if i % 2 == 0 else i + 1) % sides) for i in range(sides)])
    near = lax.ppermute(near, "tile", [(i, i ^ 1) for i in range(sides)])

    tall = width + 4 * HALO
    state = shape((groups, NZ, tall, lanes), f32)
    faces = shape((NZ, tall, lanes), f32)
    work = (state, state, faces, faces, faces, shape((COEFS, tall, lanes), f32), shape((2, tall, lanes), f32))
    begun = pl.pallas_call(
        functools.partial(begin_kernel, rows),
        out_shape=work,
        in_specs=vmem(2),
        out_specs=tuple(vmem(WORK)),
        compiler_params=params,
    )(*close(start, coefs))
    ended = pl.pallas_call(
        functools.partial(diffuse_kernel, count, rows, sides),
        out_shape=(
            shape((2, NZ, ROWS, width), f32),
            *(shape((2, NZ + 1, ROWS, width), jnp.int16) for _ in range(1, half)),
            *work,
        ),
        in_specs=vmem(3 + WORK),
        out_specs=tuple(vmem(half + WORK)),
        scratch_shapes=[pltpu.VMEM((groups, NZ, width, lanes), f32), pltpu.VMEM((NZ, rows, width), f32)],
        input_output_aliases={3 + k: half + k for k in range(WORK)},
        compiler_params=params,
    )(*close(fields, near, far, *begun))
    parts = ended[:half]

    kept, sent = pl.pallas_call(
        functools.partial(gather_kernel, half),
        out_shape=(shape((NZ * ROWS, width), f32),) * 2,
        in_specs=vmem(half),
        out_specs=tuple(vmem(2)),
    )(*close(parts[0], *(swap(parts[k], k) for k in range(1, half))))
    total = (kept + swap(sent, half)) * factor
    return total.reshape(NZ, ROWS, width)


def solution(mesh):
    flat = P("mem", "tile")
    deep = P(None, "mem", "tile")
    return jax.shard_map(
        local,
        mesh=mesh,
        in_specs=(P("mem", None, None, "tile"), deep, flat, flat, flat, flat, flat, flat),
        out_specs=deep,
        check_vma=False,
    )
```
